32 devices in a mesh: tm: 2 (over x), sx: 4 (over z), sy: 4 (over y, core).
Axes of the slice: x: 2, y: 2, z: 4, core: 2. Of those that a mesh axis runs over, the one named last changes fastest.
Arguments:
- heat_source: float32 [8, 64, 64, 128], P('tm', 'sx', 'sy'), may hold values from -8 to 8
- conductivity: float32 [64, 64, 128], P('sx', 'sy'), may hold values from 0.001 to 0.5
- initial_iterate: float32 [8, 64, 64, 128], P('tm', 'sx', 'sy'), may hold values from -6 to 6
Outputs:
- solution: float32 [8, 64, 64, 128], P('tm', 'sx', 'sy')
- residual: float32 [8, 64, 64, 128], P('tm', 'sx', 'sy')
The draws below stay inside these ranges and needn't reach their ends.
All inputs are finite; a program needn't handle non-finite values.
Results may differ from the reference program's by a relative error of at most 0.000074.
Values sent between devices are 32-bit elements; how exact they have to be, the bound alone decides.
A program may use at most 64 MiB of HBM per device.

```python
import jax
import jax.numpy as jnp
from jax import lax

STEPS = 4
NT = 8
NX = 64
NY = 64
NZ = 128


def draw_heat_source(key, part):
    rough = jax.random.normal(key, (NT, NX, NY, NZ), jnp.float32)
    return jnp.clip(rough, -8.0, 8.0)


def draw_conductivity(key, part):
    region_key = jax.random.fold_in(key, 13)
    high_key = jax.random.fold_in(key, 11)
    low_key = jax.random.fold_in(key, 12)
    regions_x = (NX + 2) // 4 + 1
    regions_y = (NY + 2) // 4 + 1
    flags = jax.random.randint(region_key, (regions_x, regions_y), 0, 2)
    index_x = ((jnp.arange(NX) + 2) // 4).astype(jnp.int32)
    index_y = ((jnp.arange(NY) + 2) // 4).astype(jnp.int32)
    low_cells = jnp.take(jnp.take(flags, index_x, axis=0), index_y, axis=1)
    high = jnp.exp(jax.random.uniform(high_key, (NX, NY, NZ), jnp.float32, jnp.log(0.02), jnp.log(0.5)))
    low = jnp.exp(jax.random.uniform(low_key, (NX, NY, NZ), jnp.float32, jnp.log(0.001), jnp.log(0.004)))
    return jnp.clip(jnp.where(low_cells[:, :, None] == 1, low, high), 0.001, 0.5)


def block_levels(key, dims, cuts, low, top_value):
    loudness, own = 1.0, jax.random.fold_in(key, 6)
    for axis_at, blocks in cuts:
        draws = jnp.exp(jax.random.uniform(jax.random.fold_in(own, axis_at), (blocks,), jnp.float32, low / len(cuts), top_value / len(cuts)))
        loudness = loudness * jnp.repeat(draws, dims[axis_at] // blocks).reshape([-1 if axis == axis_at else 1 for axis in range(len(dims))])
    return loudness


def gaussian(rng, extent, width, reach, cuts=(), dtype=jnp.bfloat16):
    values = jax.random.normal(rng, extent, jnp.float32) * width
    if len(cuts) > 0:
        values = block_levels(rng, extent, cuts, -0.22, 0.18) * values
    return jnp.clip(values, min=-reach, max=reach).astype(dtype)


def setup_inputs(seed: int = 0) -> dict:
    key_list = jax.random.split(jax.random.key(seed), 4)
    return {
        "heat_source": draw_heat_source(jax.random.fold_in(key_list[3], 71), 0),
        "conductivity": draw_conductivity(jax.random.fold_in(key_list[3], 71), 0),
        "initial_iterate": gaussian(key_list[2], (NT, NX, NY, NZ), 1.0, 6.0, ((0, 2), (1, 4), (2, 4)), jnp.float32),
    }


relax_weight = 0.8
fine_step = 1.0


def face_terms(conductivity):
    padded = jnp.pad(conductivity, 1)
    center = conductivity
    couple = (0.5 * (center + padded[2:, 1:-1, 1:-1]), 0.5 * (center + padded[:-2, 1:-1, 1:-1]),
              0.5 * (center + padded[1:-1, 2:, 1:-1]), 0.5 * (center + padded[1:-1, :-2, 1:-1]),
              0.5 * (center + padded[1:-1, 1:-1, 2:]), 0.5 * (center + padded[1:-1, 1:-1, :-2]))
    coupling = couple[0] + couple[1] + couple[2] + couple[3] + couple[4] + couple[5]
    return couple, coupling


def combine_neighbours(values, padded, couple, coupling, tau_step):
    beside = couple[0] * padded[:, 2:, 1:-1, 1:-1] + couple[1] * padded[:, :-2, 1:-1, 1:-1]
    beside = beside + couple[2] * padded[:, 1:-1, 2:, 1:-1] + couple[3] * padded[:, 1:-1, :-2, 1:-1]
    beside = beside + couple[4] * padded[:, 1:-1, 1:-1, 2:] + couple[5] * padded[:, 1:-1, 1:-1, :-2]
    return (1.0 + tau_step * coupling) * values - tau_step * beside


def apply_operator(values, couple, coupling, tau_step):
    padded = jnp.pad(values, ((0, 0), (1, 1), (1, 1), (1, 1)))
    return combine_neighbours(values, padded, couple, coupling, tau_step)


def smooth(values, source, couple, coupling, tau_step, block_len):
    diagonal = 1.0 + tau_step * coupling
    factor = relax_weight / diagonal
    applied = apply_operator(values, couple, coupling, tau_step)
    update = values + relax_weight * (source - applied) / diagonal
    earlier = jnp.concatenate([jnp.zeros_like(values[:1]), values[:-1]], axis=0)
    groups = values.shape[0] // block_len
    shaped = update.reshape((groups, block_len) + values.shape[1:])
    running = earlier.reshape((groups, block_len) + values.shape[1:])[:, 0]
    results = []
    for position in range(block_len):
        running = shaped[:, position] + factor * running
        results.append(running)
    return jnp.stack(results, axis=1).reshape(values.shape)


def defect(values, source, couple, coupling, tau_step):
    earlier = jnp.concatenate([jnp.zeros_like(values[:1]), values[:-1]], axis=0)
    return source + earlier - apply_operator(values, couple, coupling, tau_step)


def coarse_sweep(values, source, couple, coupling, tau_step):
    diagonal = 1.0 + tau_step * coupling
    factor = relax_weight / diagonal
    applied = apply_operator(values, couple, coupling, tau_step)
    update = values + relax_weight * (source - applied) / diagonal

    def advance(running, term):
        fresh_value = term + factor * running
        return fresh_value, fresh_value

    _, result = lax.scan(advance, jnp.zeros_like(values[0]), update)
    return result


def reference(heat_source, conductivity, initial_iterate):
    couple, coupling = face_terms(conductivity)
    first = smooth(initial_iterate, heat_source, couple, coupling, fine_step, STEPS)
    defect_fine = defect(first, heat_source, couple, coupling, fine_step)
    source_one = defect_fine[0::2] + defect_fine[1::2]
    error_one = smooth(jnp.zeros_like(source_one), source_one, couple, coupling, 2.0 * fine_step, STEPS // 2)
    defect_one = defect(error_one, source_one, couple, coupling, 2.0 * fine_step)
    source_two = defect_one[0::2] + defect_one[1::2]
    error_two = smooth(jnp.zeros_like(source_two), source_two, couple, coupling, 4.0 * fine_step, 1)
    defect_two = defect(error_two, source_two, couple, coupling, 4.0 * fine_step)
    source_three = defect_two[0::2] + defect_two[1::2]
    error_three = coarse_sweep(jnp.zeros_like(source_three), source_three, couple, coupling, 8.0 * fine_step)
    error_three = coarse_sweep(error_three, source_three, couple, coupling, 8.0 * fine_step)
    error_two = smooth(error_two + jnp.repeat(error_three, 2, axis=0), source_two, couple, coupling, 4.0 * fine_step, 1)
    error_one = smooth(error_one + jnp.repeat(error_two, 2, axis=0), source_one, couple, coupling, 2.0 * fine_step, STEPS // 2)
    solution = smooth(first + jnp.repeat(error_one, 2, axis=0), heat_source, couple, coupling, fine_step, STEPS)
    return solution, defect(solution, heat_source, couple, coupling, fine_step)
```

```python
import functools

import jax
import jax.numpy as jnp
from jax import lax
from jax.experimental import pallas as pl
from jax.experimental.pallas import tpu as pltpu
from jax.sharding import PartitionSpec as P

relax_weight = 0.8
keep_weight = 1.0 - relax_weight
MESH = pl.DeviceIdType.MESH

KAPPA, INIT, FIRST, ERR1, ERR2, ERR3, FIX2, FIX1, SUM0, SOL = range(10)
P_INIT, P_FIRST, P_ERR1, P_ERR2, P_FIX1, P_SUM0, P_SOL = range(7)
XLO, XHI, YLO, YHI = range(4)


def kernel(n_tm, n_sx, n_sy, unroll, hs_hbm, k_hbm, in_hbm, sol_hbm, res_hbm, *scratch):
    fields = scratch[:10]
    yrecv = scratch[10:20]
    ysend = scratch[20:30]
    (hs, res, before, second, rhs1, rhs2, rhs3, mine, theirs, chain,
     face, coupling, factor, send_sem, recv_sem, tsend, trecv,
     qsend, qrecv, csend, crecv, local) = scratch[30:]
    steps, nx, ny, nz = hs.shape
    tm, sx, sy = lax.axis_index("tm"), lax.axis_index("sx"), lax.axis_index("sy")
    has = (sx > 0, sx < n_sx - 1, sy > 0, sy < n_sy - 1)
    partner = tm + 1 - 2 * lax.rem(tm, 2)
    even = lax.rem(tm, 2) == 0

    loads = [
        pltpu.make_async_copy(k_hbm, fields[KAPPA].at[0, pl.ds(1, nx)], local.at[0]),
        pltpu.make_async_copy(in_hbm, fields[INIT].at[:, pl.ds(1, nx)], local.at[1]),
        pltpu.make_async_copy(hs_hbm, hs, local.at[2]),
    ]
    for load in loads:
        load.start()

    barrier = pltpu.get_barrier_semaphore()
    greet = [
        (has[XLO], {"sx": sx - 1}), (has[XHI], {"sx": sx + 1}),
        (has[YLO], {"sy": sy - 1}), (has[YHI], {"sy": sy + 1}),
        (tm > 0, {"tm": tm - 1}), (tm < n_tm - 1, {"tm": tm + 1}),
    ]
    if n_tm > 2:
        greet += [(tm > 1, {"tm": tm - 2}), (tm < n_tm - 2, {"tm": tm + 2})]
    count = jnp.int32(0)
    for there, device in greet:
        count = count + jnp.where(there, 1, 0)

        @pl.when(there)
        def _(device=device):
            pl.semaphore_signal(barrier, inc=1, device_id=device, device_id_type=MESH)

    pl.semaphore_wait(barrier, count)

    def face_copy(i, side):
        field = fields[i]
        if side == XLO:
            if i == INIT:
                src = in_hbm.at[:, pl.ds(0, 1)]
            elif i == KAPPA:
                src = k_hbm.at[pl.ds(0, 1)]
            else:
                src = field.at[:, pl.ds(1, 1)]
            dst, device = field.at[:, pl.ds(nx + 1, 1)], {"sx": sx - 1}
        elif side == XHI:
            if i == INIT:
                src = in_hbm.at[:, pl.ds(nx - 1, 1)]
            elif i == KAPPA:
                src = k_hbm.at[pl.ds(nx - 1, 1)]
            else:
                src = field.at[:, pl.ds(nx, 1)]
            dst, device = field.at[:, pl.ds(0, 1)], {"sx": sx + 1}
        elif side == YLO:
            src, dst, device = ysend[i].at[0], yrecv[i].at[1], {"sy": sy - 1}
        else:
            src, dst, device = ysend[i].at[1], yrecv[i].at[0], {"sy": sy + 1}
        if i == KAPPA and side in (XLO, XHI):
            dst = field.at[0, pl.ds(nx + 1 if side == XLO else 0, 1)]
        return pltpu.make_async_remote_copy(
            src_ref=src, dst_ref=dst, send_sem=send_sem.at[i, side],
            recv_sem=recv_sem.at[i, side], device_id=device, device_id_type=MESH)

    def send_faces(i, sides=(XLO, XHI, YLO, YHI)):
        for side in sides:
            @pl.when(has[side])
            def _(side=side):
                face_copy(i, side).start()

    def wait_faces(i):
        for side in (XLO, XHI, YLO, YHI):
            @pl.when(has[side ^ 1])
            def _(side=side):
                face_copy(i, side).wait_recv()

    def last_copy(i, field):
        if i == P_INIT:
            src = in_hbm.at[steps - 1]
        else:
            src = field.at[field.shape[0] - 1, pl.ds(1, nx)]
        return pltpu.make_async_remote_copy(
            src_ref=src, dst_ref=before.at[i], send_sem=tsend.at[i], recv_sem=trecv.at[i],
            device_id={"tm": tm + 1}, device_id_type=MESH)

    lasts = (INIT, FIRST, ERR1, ERR2, FIX1, SUM0, SOL)

    def send_last(i):
        @pl.when(tm < n_tm - 1)
        def _():
            last_copy(i, fields[lasts[i]]).start()

    def wait_last(i):
        @pl.when(tm > 0)
        def _():
            last_copy(i, fields[lasts[i]]).wait_recv()

    send_faces(KAPPA, (XLO, XHI))
    send_faces(INIT, (XLO, XHI))
    send_last(P_INIT)

    def over_rows(body, by=unroll):
        def step(x, carry):
            body(x)
            return carry

        lax.fori_loop(0, nx, step, 0, unroll=by)

    def put_faces(i, t, x, value):
        ysend[i][0, t, pl.ds(x, 1), :] = value[0:1, :]
        ysend[i][1, t, pl.ds(x, 1), :] = value[ny - 1:ny, :]

    def put(i, t, x, value):
        fields[i][t, x + 1] = value
        put_faces(i, t, x, value)

    loads[0].wait()
    loads[1].wait()

    def pack(x):
        put_faces(KAPPA, 0, x, fields[KAPPA][0, x + 1])
        for t in range(steps):
            put_faces(INIT, t, x, fields[INIT][t, x + 1])

    over_rows(pack)
    send_faces(KAPPA, (YLO, YHI))
    send_faces(INIT, (YLO, YHI))

    @pl.when(sx == 0)
    def _():
        for i in range(10):
            for t in range(fields[i].shape[0]):
                fields[i][t, 0] = jnp.zeros((ny, nz), jnp.float32)

    @pl.when(sx == n_sx - 1)
    def _():
        for i in range(10):
            for t in range(fields[i].shape[0]):
                fields[i][t, nx + 1] = jnp.zeros((ny, nz), jnp.float32)

    @pl.when(sy == 0)
    def _():
        for i in range(10):
            yrecv[i][0] = jnp.zeros(yrecv[i].shape[1:], jnp.float32)

    @pl.when(sy == n_sy - 1)
    def _():
        for i in range(10):
            yrecv[i][1] = jnp.zeros(yrecv[i].shape[1:], jnp.float32)

    @pl.when(tm == 0)
    def _():
        def clear(x):
            for i in range(7):
                before[i, x] = jnp.zeros((ny, nz), jnp.float32)

        over_rows(clear, 1)

    row = lax.broadcasted_iota(jnp.int32, (ny, nz), 0)
    column = lax.broadcasted_iota(jnp.int32, (ny, nz), 1)

    def around(i, t, x):
        field = fields[i]
        here = field[t, x + 1]
        return here, (
            field[t, x + 2],
            field[t, x],
            jnp.where(row == ny - 1, yrecv[i][1, t, pl.ds(x, 1), :], pltpu.roll(here, ny - 1, 0)),
            jnp.where(row == 0, yrecv[i][0, t, pl.ds(x, 1), :], pltpu.roll(here, 1, 0)),
            pltpu.roll(here, nz - 1, 1),
            pltpu.roll(here, 1, 1),
        )

    def beside(i, t, x, g):
        here, sides = around(i, t, x)
        terms = [g[j] * sides[j] for j in range(6)]
        return here, (terms[0] + terms[1]) + (terms[2] + terms[3]) + (terms[4] + terms[5])

    def faces_at(x):
        return [face[j, x] for j in range(6)]

    wait_faces(KAPPA)

    def coefficients(x):
        here, sides = around(KAPPA, 0, x)
        sides = list(sides)
        sides[4] = jnp.where(column == nz - 1, 0.0, sides[4])
        sides[5] = jnp.where(column == 0, 0.0, sides[5])
        g = [0.5 * (here + side) for side in sides]
        total = (g[0] + g[1]) + (g[2] + g[3]) + (g[4] + g[5])
        coupling[x] = total
        g[4] = jnp.where(column == nz - 1, 0.0, g[4])
        g[5] = jnp.where(column == 0, 0.0, g[5])
        for j in range(6):
            face[j, x] = g[j]
        for level in range(4):
            factor[level, x] = relax_weight / (1.0 + (2.0 ** level) * total)

    over_rows(coefficients)
    loads[2].wait()
    wait_faces(INIT)
    wait_last(P_INIT)

    def sweep_first(x):
        g, f = faces_at(x), factor[0, x]
        running = before[P_INIT, x]
        for t in range(steps):
            here, near = beside(INIT, t, x, g)
            running = keep_weight * here + f * (hs[t, x] + near + running)
            put(FIRST, t, x, running)

    over_rows(sweep_first)
    send_faces(FIRST)
    send_last(P_FIRST)
    wait_faces(FIRST)
    wait_last(P_FIRST)

    def down_one(x):
        g, diagonal, f = faces_at(x), 1.0 + coupling[x], factor[1, x]
        earlier = before[P_FIRST, x]
        running = None
        for m in range(steps // 2):
            total = None
            for t in (2 * m, 2 * m + 1):
                here, near = beside(FIRST, t, x, g)
                value = hs[t, x] + earlier - (diagonal * here - near)
                total = value if total is None else total + value
                earlier = here
            rhs1[m, x] = total
            running = f * total if running is None else f * (total + running)
            put(ERR1, m, x, running)

    over_rows(down_one)
    send_faces(ERR1)
    send_last(P_ERR1)
    wait_faces(ERR1)
    wait_last(P_ERR1)

    def down_two(x):
        g, diagonal, f = faces_at(x), 1.0 + 2.0 * coupling[x], factor[2, x]
        earlier = before[P_ERR1, x]
        total = None
        for t in range(2):
            here, near = beside(ERR1, t, x, g)
            value = rhs1[t, x] + earlier - (diagonal * here - 2.0 * near)
            total = value if total is None else total + value
            earlier = here
        rhs2[x] = total
        put(ERR2, 0, x, f * total)

    over_rows(down_two)
    send_faces(ERR2)
    send_last(P_ERR2)
    wait_faces(ERR2)
    if n_tm > 2:
        wait_last(P_ERR2)

    def down_three(x):
        g, diagonal = faces_at(x), 1.0 + 4.0 * coupling[x]
        here, near = beside(ERR2, 0, x, g)
        earlier = here + before[P_ERR2, x] if n_tm > 2 else here
        mine[x] = rhs2[x] + jnp.where(even, earlier, 0.0) - (diagonal * here - 4.0 * near)

    over_rows(down_three)
    swap = pltpu.make_async_remote_copy(
        src_ref=mine, dst_ref=theirs, send_sem=qsend, recv_sem=qrecv,
        device_id={"tm": partner}, device_id_type=MESH)
    swap.start()
    swap.wait_recv()

    def chain_copy(i, field):
        src = field.at[0, pl.ds(1, nx)] if i == 0 else second
        return pltpu.make_async_remote_copy(
            src_ref=src, dst_ref=chain.at[i], send_sem=csend.at[i],
            recv_sem=crecv.at[i], device_id={"tm": tm + 2}, device_id_type=MESH)

    def chain_wait(i):
        if n_tm > 2:
            @pl.when(tm > 1)
            def _():
                chain_copy(i, fields[ERR3]).wait_recv()

            @pl.when(tm < 2)
            def _():
                def clear(x):
                    chain[i, x] = jnp.zeros((ny, nz), jnp.float32)

                over_rows(clear, 1)

    def chain_send(i):
        if n_tm > 2:
            @pl.when(tm < n_tm - 2)
            def _():
                chain_copy(i, fields[ERR3]).start()

    chain_wait(0)

    def coarse_one(x):
        total = mine[x] + theirs[x]
        rhs3[x] = total
        if n_tm > 2:
            total = total + chain[0, x]
        put(ERR3, 0, x, factor[3, x] * total)

    over_rows(coarse_one)
    send_faces(ERR3)
    chain_send(0)
    wait_faces(ERR3)
    if n_tm == 2:
        wait_last(P_ERR2)
    chain_wait(1)

    def coarse_two(x):
        here, near = beside(ERR3, 0, x, faces_at(x))
        total = rhs3[x] + 8.0 * near
        if n_tm > 2:
            total = total + chain[1, x]
        value = keep_weight * here + factor[3, x] * total
        if n_tm > 2:
            second[x] = value
            earlier = jnp.where(even, chain[1, x], value)
        else:
            earlier = jnp.where(even, 0.0, value)
        mine_next[x] = before[P_ERR2, x] + earlier
        put(FIX2, 0, x, fields[ERR2][0, x + 1] + value)

    mine_next = res.at[0]
    over_rows(coarse_two)
    send_faces(FIX2)
    chain_send(1)
    wait_faces(FIX2)

    def up_two(x):
        here, near = beside(FIX2, 0, x, faces_at(x))
        value = keep_weight * here + factor[2, x] * (rhs2[x] + 4.0 * near + mine_next[x])
        for m in range(2):
            put(FIX1, m, x, fields[ERR1][m, x + 1] + value)

    over_rows(up_two)
    send_faces(FIX1)
    send_last(P_FIX1)
    wait_faces(FIX1)
    wait_last(P_FIX1)

    def up_one(x):
        g, f = faces_at(x), factor[1, x]
        running = before[P_FIX1, x]
        for m in range(2):
            here, near = beside(FIX1, m, x, g)
            running = keep_weight * here + f * (rhs1[m, x] + 2.0 * near + running)
            for t in (2 * m, 2 * m + 1):
                put(SUM0, t, x, fields[FIRST][t, x + 1] + running)

    over_rows(up_one)
    send_faces(SUM0)
    send_last(P_SUM0)
    wait_faces(SUM0)
    wait_last(P_SUM0)

    def up_zero(x):
        g, f = faces_at(x), factor[0, x]
        running = before[P_SUM0, x]
        for t in range(steps):
            here, near = beside(SUM0, t, x, g)
            running = keep_weight * here + f * (hs[t, x] + near + running)
            put(SOL, t, x, running)

    over_rows(up_zero)
    send_faces(SOL)
    send_last(P_SOL)
    out_one = pltpu.make_async_copy(fields[SOL].at[:, pl.ds(1, nx)], sol_hbm, local.at[3])
    out_one.start()
    wait_faces(SOL)
    wait_last(P_SOL)

    def last_defect(x):
        g, diagonal = faces_at(x), 1.0 + coupling[x]
        earlier = before[P_SOL, x]
        for t in range(steps):
            here, near = beside(SOL, t, x, g)
            res[t, x] = hs[t, x] + earlier - (diagonal * here - near)
            earlier = here

    over_rows(last_defect)
    out_two = pltpu.make_async_copy(res, res_hbm, local.at[4])
    out_two.start()

    for i in range(10):
        for side in (XLO, XHI, YLO, YHI):
            @pl.when(has[side])
            def _(i=i, side=side):
                face_copy(i, side).wait_send()

    @pl.when(tm < n_tm - 1)
    def _():
        for i in range(7):
            last_copy(i, fields[lasts[i]]).wait_send()

    swap.wait_send()
    if n_tm > 2:
        @pl.when(tm < n_tm - 2)
        def _():
            for i in range(2):
                chain_copy(i, fields[ERR3]).wait_send()

    out_one.wait()
    out_two.wait()


def solution(mesh):
    n_tm, n_sx, n_sy = (mesh.shape[axis] for axis in ("tm", "sx", "sy"))
    f32 = jnp.float32

    def per_device(heat_source, conductivity, initial_iterate):
        steps, nx, ny, nz = heat_source.shape
        depth = (1, steps, steps, steps // 2, 1, 1, 1, steps // 2, steps, steps)
        scratch = [pltpu.VMEM((d, nx + 2, ny, nz), f32) for d in depth]
        scratch += [pltpu.VMEM((2, d, nx, nz), f32) for d in depth] * 2
        cells = (nx, ny, nz)
        dma = pltpu.SemaphoreType.DMA
        scratch += [
            pltpu.VMEM((steps,) + cells, f32),
            pltpu.VMEM((steps,) + cells, f32),
            pltpu.VMEM((7,) + cells, f32),
            pltpu.VMEM(cells, f32),
            pltpu.VMEM((steps // 2,) + cells, f32),
            pltpu.VMEM(cells, f32),
            pltpu.VMEM(cells, f32),
            pltpu.VMEM(cells, f32),
            pltpu.VMEM(cells, f32),
            pltpu.VMEM((2,) + cells, f32),
            pltpu.VMEM((6,) + cells, f32),
            pltpu.VMEM(cells, f32),
            pltpu.VMEM((4,) + cells, f32),
            dma((10, 4)), dma((10, 4)), dma((7,)), dma((7,)),
            dma, dma, dma((2,)), dma((2,)), dma((5,)),
        ]
        field = jax.ShapeDtypeStruct(heat_source.shape, f32)
        return pl.pallas_call(
            functools.partial(kernel, n_tm, n_sx, n_sy, 2),
            out_shape=(field, field),
            in_specs=[pl.BlockSpec(memory_space=pl.ANY)] * 3,
            out_specs=(pl.BlockSpec(memory_space=pl.ANY),) * 2,
            scratch_shapes=scratch,
            compiler_params=pltpu.CompilerParams(
                collective_id=0, has_side_effects=True, vmem_limit_bytes=40 * 2 ** 20
            ),
            name="vcycle",
        )(heat_source, conductivity, initial_iterate)

    placed = (P("tm", "sx", "sy", None), P("sx", "sy", None), P("tm", "sx", "sy", None))
    return jax.shard_map(
        per_device,
        mesh=mesh,
        in_specs=placed,
        out_specs=(P("tm", "sx", "sy", None), P("tm", "sx", "sy", None)),
        check_vma=False,
    )
```

```python
import functools

import jax
import jax.numpy as jnp
from jax import lax
from jax.experimental import pallas as pl
from jax.experimental.pallas import tpu as pltpu
from jax.sharding import PartitionSpec as P

relax_weight = 0.8
keep_weight = 1.0 - relax_weight
MESH = pl.DeviceIdType.MESH

KAPPA, INIT, FIRST, ERR1, ERR2, ERR3, FIX2, FIX1, SUM0, SOL = range(10)
P_INIT, P_FIRST, P_ERR1, P_ERR2, P_FIX1, P_SUM0, P_SOL = range(7)
XLO, XHI, YLO, YHI = range(4)


def kernel(n_tm, n_sx, n_sy, unroll, hs_hbm, k_hbm, in_hbm, sol_hbm, res_hbm, *scratch):
    fields = scratch[:10]
    yrecv = scratch[10:20]
    ysend = scratch[20:30]
    (hs, res, before, second, rhs1, rhs2, rhs3, mine, theirs, chain,
     face, coupling, factor, send_sem, recv_sem, tsend, trecv,
     qsend, qrecv, csend, crecv, local) = scratch[30:]
    steps, nx, ny, nz = hs.shape
    tm, sx, sy = lax.axis_index("tm"), lax.axis_index("sx"), lax.axis_index("sy")
    has = (sx > 0, sx < n_sx - 1, sy > 0, sy < n_sy - 1)
    partner = tm + 1 - 2 * lax.rem(tm, 2)
    even = lax.rem(tm, 2) == 0

    loads = [
        pltpu.make_async_copy(k_hbm, fields[KAPPA].at[0, pl.ds(1, nx)], local.at[0]),
        pltpu.make_async_copy(in_hbm, fields[INIT].at[:, pl.ds(1, nx)], local.at[1]),
        pltpu.make_async_copy(hs_hbm, hs, local.at[2]),
    ]
    for load in loads:
        load.start()

    barrier = pltpu.get_barrier_semaphore()
    greet = [
        (has[XLO], {"sx": sx - 1}), (has[XHI], {"sx": sx + 1}),
        (has[YLO], {"sy": sy - 1}), (has[YHI], {"sy": sy + 1}),
        (tm > 0, {"tm": tm - 1}), (tm < n_tm - 1, {"tm": tm + 1}),
    ]
    if n_tm > 2:
        greet += [(tm > 1, {"tm": tm - 2}), (tm < n_tm - 2, {"tm": tm + 2})]
    count = jnp.int32(0)
    for there, device in greet:
        count = count + jnp.where(there, 1, 0)

        @pl.when(there)
        def _(device=device):
            pl.semaphore_signal(barrier, inc=1, device_id=device, device_id_type=MESH)

    pl.semaphore_wait(barrier, count)

    def face_copy(i, side):
        field = fields[i]
        if side == XLO:
            if i == INIT:
                src = in_hbm.at[:, pl.ds(0, 1)]
            elif i == KAPPA:
                src = k_hbm.at[pl.ds(0, 1)]
            else:
                src = field.at[:, pl.ds(1, 1)]
            dst, device = field.at[:, pl.ds(nx + 1, 1)], {"sx": sx - 1}
        elif side == XHI:
            if i == INIT:
                src = in_hbm.at[:, pl.ds(nx - 1, 1)]
            elif i == KAPPA:
                src = k_hbm.at[pl.ds(nx - 1, 1)]
            else:
                src = field.at[:, pl.ds(nx, 1)]
            dst, device = field.at[:, pl.ds(0, 1)], {"sx": sx + 1}
        elif side == YLO:
            src, dst, device = ysend[i].at[0], yrecv[i].at[1], {"sy": sy - 1}
        else:
            src, dst, device = ysend[i].at[1], yrecv[i].at[0], {"sy": sy + 1}
        if i == KAPPA and side in (XLO, XHI):
            dst = field.at[0, pl.ds(nx + 1 if side == XLO else 0, 1)]
        return pltpu.make_async_remote_copy(
            src_ref=src, dst_ref=dst, send_sem=send_sem.at[i, side],
            recv_sem=recv_sem.at[i, side], device_id=device, device_id_type=MESH)

    def send_faces(i, sides=(XLO, XHI, YLO, YHI)):
        for side in sides:
            @pl.when(has[side])
            def _(side=side):
                face_copy(i, side).start()

    def wait_faces(i):
        for side in (XLO, XHI, YLO, YHI):
            @pl.when(has[side ^ 1])
            def _(side=side):
                face_copy(i, side).wait_recv()

    def last_copy(i, field):
        if i == P_INIT:
            src = in_hbm.at[steps - 1]
        else:
            src = field.at[field.shape[0] - 1, pl.ds(1, nx)]
        return pltpu.make_async_remote_copy(
            src_ref=src, dst_ref=before.at[i], send_sem=tsend.at[i], recv_sem=trecv.at[i],
            device_id={"tm": tm + 1}, device_id_type=MESH)

    lasts = (INIT, FIRST, ERR1, ERR2, FIX1, SUM0, SOL)

    def send_last(i):
        @pl.when(tm < n_tm - 1)
        def _():
            last_copy(i, fields[lasts[i]]).start()

    def wait_last(i):
        @pl.when(tm > 0)
        def _():
            last_copy(i, fields[lasts[i]]).wait_recv()

    send_faces(KAPPA, (XLO, XHI))
    send_faces(INIT, (XLO, XHI))
    send_last(P_INIT)

    def over_rows(body, by=unroll):
        def step(x, carry):
            body(x)
            return carry

        lax.fori_loop(0, nx, step, 0, unroll=by)

    def put_faces(i, t, x, value):
        ysend[i][0, t, pl.ds(x, 1), :] = value[0:1, :]
        ysend[i][1, t, pl.ds(x, 1), :] = value[ny - 1:ny, :]

    def put(i, t, x, value):
        fields[i][t, x + 1] = value
        put_faces(i, t, x, value)

    loads[0].wait()
    loads[1].wait()

    def pack(x):
        put_faces(KAPPA, 0, x, fields[KAPPA][0, x + 1])
        for t in range(steps):
            put_faces(INIT, t, x, fields[INIT][t, x + 1])

    over_rows(pack)
    send_faces(KAPPA, (YLO, YHI))
    send_faces(INIT, (YLO, YHI))

    @pl.when(sx == 0)
    def _():
        for i in range(10):
            for t in range(fields[i].shape[0]):
                fields[i][t, 0] = jnp.zeros((ny, nz), jnp.float32)

    @pl.when(sx == n_sx - 1)
    def _():
        for i in range(10):
            for t in range(fields[i].shape[0]):
                fields[i][t, nx + 1] = jnp.zeros((ny, nz), jnp.float32)

    @pl.when(sy == 0)
    def _():
        for i in range(10):
            yrecv[i][0] = jnp.zeros(yrecv[i].shape[1:], jnp.float32)

    @pl.when(sy == n_sy - 1)
    def _():
        for i in range(10):
            yrecv[i][1] = jnp.zeros(yrecv[i].shape[1:], jnp.float32)

    @pl.when(tm == 0)
    def _():
        def clear(x):
            for i in range(7):
                before[i, x] = jnp.zeros((ny, nz), jnp.float32)

        over_rows(clear, 1)

    row = lax.broadcasted_iota(jnp.int32, (ny, nz), 0)
    column = lax.broadcasted_iota(jnp.int32, (ny, nz), 1)

    def around(i, t, x):
        field = fields[i]
        here = field[t, x + 1]
        return here, (
            field[t, x + 2],
            field[t, x],
            jnp.where(row == ny - 1, yrecv[i][1, t, pl.ds(x, 1), :], pltpu.roll(here, ny - 1, 0)),
            jnp.where(row == 0, yrecv[i][0, t, pl.ds(x, 1), :], pltpu.roll(here, 1, 0)),
            pltpu.roll(here, nz - 1, 1),
            pltpu.roll(here, 1, 1),
        )

    def beside(i, t, x, g):
        here, sides = around(i, t, x)
        terms = [g[j] * sides[j] for j in range(6)]
        return here, (terms[0] + terms[1]) + (terms[2] + terms[3]) + (terms[4] + terms[5])

    def faces_at(x):
        return [face[j, x] for j in range(6)]

    wait_faces(KAPPA)

    def coefficients(x):
        here, sides = around(KAPPA, 0, x)
        sides = list(sides)
        sides[4] = jnp.where(column == nz - 1, 0.0, sides[4])
        sides[5] = jnp.where(column == 0, 0.0, sides[5])
        g = [0.5 * (here + side) for side in sides]
        total = (g[0] + g[1]) + (g[2] + g[3]) + (g[4] + g[5])
        coupling[x] = total
        g[4] = jnp.where(column == nz - 1, 0.0, g[4])
        g[5] = jnp.where(column == 0, 0.0, g[5])
        for j in range(6):
            face[j, x] = g[j]
        for level in range(4):
            factor[level, x] = relax_weight / (1.0 + (2.0 ** level) * total)

    over_rows(coefficients)
    loads[2].wait()
    wait_faces(INIT)
    wait_last(P_INIT)

    def sweep_first(x):
        g, f = faces_at(x), factor[0, x]
        running = before[P_INIT, x]
        for t in range(steps):
            here, near = beside(INIT, t, x, g)
            running = keep_weight * here + f * (hs[t, x] + near + running)
            put(FIRST, t, x, running)

    over_rows(sweep_first)
    send_faces(FIRST)
    send_last(P_FIRST)
    wait_faces(FIRST)
    wait_last(P_FIRST)

    def down_one(x):
        g, diagonal, f = faces_at(x), 1.0 + coupling[x], factor[1, x]
        earlier = before[P_FIRST, x]
        running = None
        for m in range(steps // 2):
            total = None
            for t in (2 * m, 2 * m + 1):
                here, near = beside(FIRST, t, x, g)
                value = hs[t, x] + earlier - (diagonal * here - near)
                total = value if total is None else total + value
                earlier = here
            rhs1[m, x] = total
            running = f * total if running is None else f * (total + running)
            put(ERR1, m, x, running)

    over_rows(down_one)
    send_faces(ERR1)
    send_last(P_ERR1)
    wait_faces(ERR1)
    wait_last(P_ERR1)

    def down_two(x):
        g, diagonal, f = faces_at(x), 1.0 + 2.0 * coupling[x], factor[2, x]
        earlier = before[P_ERR1, x]
        total = None
        for t in range(2):
            here, near = beside(ERR1, t, x, g)
            value = rhs1[t, x] + earlier - (diagonal * here - 2.0 * near)
            total = value if total is None else total + value
            earlier = here
        rhs2[x] = total
        put(ERR2, 0, x, f * total)

    over_rows(down_two)
    send_faces(ERR2)
    send_last(P_ERR2)
    wait_faces(ERR2)
    if n_tm > 2:
        wait_last(P_ERR2)

    def down_three(x):
        g, diagonal = faces_at(x), 1.0 + 4.0 * coupling[x]
        here, near = beside(ERR2, 0, x, g)
        earlier = here + before[P_ERR2, x] if n_tm > 2 else here
        mine[x] = rhs2[x] + jnp.where(even, earlier, 0.0) - (diagonal * here - 4.0 * near)

    over_rows(down_three)
    swap = pltpu.make_async_remote_copy(
        src_ref=mine, dst_ref=theirs, send_sem=qsend, recv_sem=qrecv,
        device_id={"tm": partner}, device_id_type=MESH)
    swap.start()
    swap.wait_recv()

    def chain_copy(i, field):
        src = field.at[0, pl.ds(1, nx)] if i == 0 else second
        return pltpu.make_async_remote_copy(
            src_ref=src, dst_ref=chain.at[i], send_sem=csend.at[i],
            recv_sem=crecv.at[i], device_id={"tm": tm + 2}, device_id_type=MESH)

    def chain_wait(i):
        if n_tm > 2:
            @pl.when(tm > 1)
            def _():
                chain_copy(i, fields[ERR3]).wait_recv()

            @pl.when(tm < 2)
            def _():
                def clear(x):
                    chain[i, x] = jnp.zeros((ny, nz), jnp.float32)

                over_rows(clear, 1)

    def chain_send(i):
        if n_tm > 2:
            @pl.when(tm < n_tm - 2)
            def _():
                chain_copy(i, fields[ERR3]).start()

    chain_wait(0)

    def coarse_one(x):
        total = mine[x] + theirs[x]
        rhs3[x] = total
        if n_tm > 2:
            total = total + chain[0, x]
        put(ERR3, 0, x, factor[3, x] * total)

    over_rows(coarse_one)
    send_faces(ERR3)
    chain_send(0)
    wait_faces(ERR3)
    if n_tm == 2:
        wait_last(P_ERR2)
    chain_wait(1)

    def coarse_two(x):
        here, near = beside(ERR3, 0, x, faces_at(x))
        total = rhs3[x] + 8.0 * near
        if n_tm > 2:
            total = total + chain[1, x]
        value = keep_weight * here + factor[3, x] * total
        if n_tm > 2:
            second[x] = value
            earlier = jnp.where(even, chain[1, x], value)
        else:
            earlier = jnp.where(even, 0.0, value)
        mine_next[x] = before[P_ERR2, x] + earlier
        put(FIX2, 0, x, fields[ERR2][0, x + 1] + value)

    mine_next = res.at[0]
    over_rows(coarse_two)
    send_faces(FIX2)
    chain_send(1)
    wait_faces(FIX2)

    def up_two(x):
        here, near = beside(FIX2, 0, x, faces_at(x))
        value = keep_weight * here + factor[2, x] * (rhs2[x] + 4.0 * near + mine_next[x])
        for m in range(2):
            put(FIX1, m, x, fields[ERR1][m, x + 1] + value)

    over_rows(up_two)
    send_faces(FIX1)
    send_last(P_FIX1)
    wait_faces(FIX1)
    wait_last(P_FIX1)

    def up_one(x):
        g, f = faces_at(x), factor[1, x]
        running = before[P_FIX1, x]
        for m in range(2):
            here, near = beside(FIX1, m, x, g)
            running = keep_weight * here + f * (rhs1[m, x] + 2.0 * near + running)
            for t in (2 * m, 2 * m + 1):
                put(SUM0, t, x, fields[FIRST][t, x + 1] + running)

    over_rows(up_one)
    send_faces(SUM0)
    send_last(P_SUM0)
    wait_faces(SUM0)
    wait_last(P_SUM0)

    def up_zero(x):
        g, f = faces_at(x), factor[0, x]
        running = before[P_SUM0, x]
        for t in range(steps):
            here, near = beside(SUM0, t, x, g)
            running = keep_weight * here + f * (hs[t, x] + near + running)
            put(SOL, t, x, running)

    over_rows(up_zero)
    send_faces(SOL)
    send_last(P_SOL)
    out_one = pltpu.make_async_copy(fields[SOL].at[:, pl.ds(1, nx)], sol_hbm, local.at[3])
    out_one.start()
    wait_faces(SOL)
    wait_last(P_SOL)

    def last_defect(x):
        g, diagonal = faces_at(x), 1.0 + coupling[x]
        earlier = before[P_SOL, x]
        for t in range(steps):
            here, near = beside(SOL, t, x, g)
            res[t, x] = hs[t, x] + earlier - (diagonal * here - near)
            earlier = here

    over_rows(last_defect)
    out_two = pltpu.make_async_copy(res, res_hbm, local.at[4])
    out_two.start()

    for i in range(10):
        for side in (XLO, XHI, YLO, YHI):
            @pl.when(has[side])
            def _(i=i, side=side):
                face_copy(i, side).wait_send()

    @pl.when(tm < n_tm - 1)
    def _():
        for i in range(7):
            last_copy(i, fields[lasts[i]]).wait_send()

    swap.wait_send()
    if n_tm > 2:
        @pl.when(tm < n_tm - 2)
        def _():
            for i in range(2):
                chain_copy(i, fields[ERR3]).wait_send()

    out_one.wait()
    out_two.wait()


def solution(mesh):
    n_tm, n_sx, n_sy = (mesh.shape[axis] for axis in ("tm", "sx", "sy"))
    f32 = jnp.float32

    def per_device(heat_source, conductivity, initial_iterate):
        steps, nx, ny, nz = heat_source.shape
        depth = (1, steps, steps, steps // 2, 1, 1, 1, steps // 2, steps, steps)
        scratch = [pltpu.VMEM((d, nx + 2, ny, nz), f32) for d in depth]
        scratch += [pltpu.VMEM((2, d, nx, nz), f32) for d in depth] * 2
        cells = (nx, ny, nz)
        dma = pltpu.SemaphoreType.DMA
        scratch += [
            pltpu.VMEM((steps,) + cells, f32),
            pltpu.VMEM((steps,) + cells, f32),
            pltpu.VMEM((7,) + cells, f32),
            pltpu.VMEM(cells, f32),
            pltpu.VMEM((steps // 2,) + cells, f32),
            pltpu.VMEM(cells, f32),
            pltpu.VMEM(cells, f32),
            pltpu.VMEM(cells, f32),
            pltpu.VMEM(cells, f32),
            pltpu.VMEM((2,) + cells, f32),
            pltpu.VMEM((6,) + cells, f32),
            pltpu.VMEM(cells, f32),
            pltpu.VMEM((4,) + cells, f32),
            dma((10, 4)), dma((10, 4)), dma((7,)), dma((7,)),
            dma, dma, dma((2,)), dma((2,)), dma((5,)),
        ]
        field = jax.ShapeDtypeStruct(heat_source.shape, f32)
        return pl.pallas_call(
            functools.partial(kernel, n_tm, n_sx, n_sy, 8),
            out_shape=(field, field),
            in_specs=[pl.BlockSpec(memory_space=pltpu.HBM)] * 3,
            out_specs=(pl.BlockSpec(memory_space=pltpu.HBM),) * 2,
            scratch_shapes=scratch,
            compiler_params=pltpu.CompilerParams(
                collective_id=0, has_side_effects=True, vmem_limit_bytes=67043328
            ),
            name="vcycle",
        )(heat_source, conductivity, initial_iterate)

    placed = (P("tm", "sx", "sy", None), P("sx", "sy", None), P("tm", "sx", "sy", None))
    return jax.shard_map(
        per_device,
        mesh=mesh,
        in_specs=placed,
        out_specs=(P("tm", "sx", "sy", None), P("tm", "sx", "sy", None)),
        check_vma=False,
    )
```

```python
import functools

import jax
import jax.numpy as jnp
from jax import lax
from jax.experimental import pallas as pl
from jax.experimental.pallas import tpu as pltpu
from jax.sharding import PartitionSpec as P

relax_weight = 0.8
keep_weight = 1.0 - relax_weight
MESH = pl.DeviceIdType.MESH

KAPPA, INIT, FIRST, ERR1, ERR2, ERR3, FIX2, FIX1, SUM0, SOL, PART, PAIR = range(12)
FIELDS = 12
P_INIT, P_FIRST, P_ERR1, P_ERR2, P_FIX1, P_SUM0, P_SOL = range(7)
XLO, XHI, YLO, YHI = range(4)


def kernel(n_tm, n_sx, n_sy, hs_hbm, k_hbm, in_hbm, sol_hbm, res_hbm, *scratch):
    fields = scratch[:FIELDS]
    yrecv = scratch[FIELDS:2 * FIELDS]
    ysend = scratch[2 * FIELDS:3 * FIELDS]
    (hs, res, before, second, rhs1, rhs2, rhs3, mine, theirs, chain,
     face, coupling, factor, send_sem, recv_sem, tsend, trecv,
     qsend, qrecv, csend, crecv, local) = scratch[3 * FIELDS:]
    steps, nx, ny, nz = hs.shape
    tm, sx, sy = lax.axis_index("tm"), lax.axis_index("sx"), lax.axis_index("sy")
    has = (sx > 0, sx < n_sx - 1, sy > 0, sy < n_sy - 1)
    partner = tm + 1 - 2 * lax.rem(tm, 2)
    even = lax.rem(tm, 2) == 0

    loads = [
        pltpu.make_async_copy(k_hbm, fields[KAPPA].at[0, pl.ds(1, nx)], local.at[0]),
        pltpu.make_async_copy(in_hbm, fields[INIT].at[:, pl.ds(1, nx)], local.at[1]),
        pltpu.make_async_copy(hs_hbm, hs, local.at[2]),
    ]
    for load in loads:
        load.start()

    barrier = pltpu.get_barrier_semaphore()
    greet = [
        (has[XLO], {"sx": sx - 1}), (has[XHI], {"sx": sx + 1}),
        (has[YLO], {"sy": sy - 1}), (has[YHI], {"sy": sy + 1}),
        (tm > 0, {"tm": tm - 1}), (tm < n_tm - 1, {"tm": tm + 1}),
    ]
    if n_tm == 2:
        greet += [
            (has[XLO], {"tm": partner, "sx": sx - 1}), (has[XHI], {"tm": partner, "sx": sx + 1}),
            (has[YLO], {"tm": partner, "sy": sy - 1}), (has[YHI], {"tm": partner, "sy": sy + 1}),
        ]
    if n_tm > 2:
        greet += [(tm > 1, {"tm": tm - 2}), (tm < n_tm - 2, {"tm": tm + 2})]
    count = jnp.int32(0)
    for there, device in greet:
        count = count + jnp.where(there, 1, 0)

        @pl.when(there)
        def _(device=device):
            pl.semaphore_signal(barrier, inc=1, device_id=device, device_id_type=MESH)

    pl.semaphore_wait(barrier, count)

    def face_copy(i, side, pair=False):
        field = fields[i]
        to = PAIR if pair else i
        land = fields[to]
        if side == XLO:
            if i == INIT:
                src = in_hbm.at[:, pl.ds(0, 1)]
            elif i == KAPPA:
                src = k_hbm.at[pl.ds(0, 1)]
            else:
                src = field.at[:, pl.ds(1, 1)]
            dst, device = land.at[:, pl.ds(nx + 1, 1)], {"sx": sx - 1}
        elif side == XHI:
            if i == INIT:
                src = in_hbm.at[:, pl.ds(nx - 1, 1)]
            elif i == KAPPA:
                src = k_hbm.at[pl.ds(nx - 1, 1)]
            else:
                src = field.at[:, pl.ds(nx, 1)]
            dst, device = land.at[:, pl.ds(0, 1)], {"sx": sx + 1}
        elif side == YLO:
            src, dst, device = ysend[i].at[0], yrecv[to].at[1], {"sy": sy - 1}
        else:
            src, dst, device = ysend[i].at[1], yrecv[to].at[0], {"sy": sy + 1}
        if i == KAPPA and side in (XLO, XHI):
            dst = field.at[0, pl.ds(nx + 1 if side == XLO else 0, 1)]
        if pair:
            device["tm"] = partner
        return pltpu.make_async_remote_copy(
            src_ref=src, dst_ref=dst, send_sem=send_sem.at[to, side],
            recv_sem=recv_sem.at[to, side], device_id=device, device_id_type=MESH)

    def send_faces(i, sides, pair=False):
        for side in sides:
            @pl.when(has[side])
            def _(side=side):
                face_copy(i, side).start()
                if pair:
                    face_copy(i, side, True).start()

    def wait_faces(i, pair=False):
        for side in (YLO, YHI, XLO, XHI):
            @pl.when(has[side ^ 1])
            def _(side=side):
                face_copy(i, side).wait_recv()
                if pair:
                    face_copy(i, side, True).wait_recv()

    half = nx // 2
    halves = (pl.ds(0, half), pl.ds(half, nx - half))

    def last_copy(i, part):
        field = fields[lasts[i]]
        if i == P_INIT:
            src = in_hbm.at[steps - 1, halves[part]]
        else:
            src = field.at[field.shape[0] - 1, (pl.ds(1, half), pl.ds(1 + half, nx - half))[part]]
        return pltpu.make_async_remote_copy(
            src_ref=src, dst_ref=before.at[i, halves[part]],
            send_sem=tsend.at[i, part], recv_sem=trecv.at[i, part],
            device_id={"tm": tm + 1}, device_id_type=MESH)

    lasts = (INIT, FIRST, ERR1, ERR2, FIX1, SUM0, SOL)

    def send_last(i, part):
        @pl.when(tm < n_tm - 1)
        def _():
            last_copy(i, part).start()

    def wait_last(i):
        @pl.when(tm > 0)
        def _():
            for part in range(2):
                last_copy(i, part).wait_recv()

    send_faces(KAPPA, (XLO, XHI))
    send_faces(INIT, (XLO, XHI))
    send_last(P_INIT, 0)
    send_last(P_INIT, 1)

    def over_rows(body, by=8, start=0, stop=nx):
        def step(x, carry):
            body(x)
            return carry

        lax.fori_loop(start, stop, step, 0, unroll=by)

    def phase(body, i, send_part=None, pair=False):
        body(0)
        body(nx - 1)
        send_faces(i, (XLO, XHI), pair)
        over_rows(body, half - 1, 1, half)
        if send_part is not None:
            send_part(0)
        over_rows(body, half - 1, half, nx - 1)
        send_faces(i, (YLO, YHI), pair)
        if send_part is not None:
            send_part(1)

    def put_faces(i, t, x, value):
        ysend[i][0, t, pl.ds(x, 1), :] = value[0:1, :]
        ysend[i][1, t, pl.ds(x, 1), :] = value[ny - 1:ny, :]

    def put(i, t, x, value):
        fields[i][t, x + 1] = value
        put_faces(i, t, x, value)

    loads[0].wait()
    loads[1].wait()

    def pack(x):
        put_faces(KAPPA, 0, x, fields[KAPPA][0, x + 1])
        for t in range(steps):
            put_faces(INIT, t, x, fields[INIT][t, x + 1])

    over_rows(pack)
    send_faces(KAPPA, (YLO, YHI))
    send_faces(INIT, (YLO, YHI))

    @pl.when(sx == 0)
    def _():
        for i in range(FIELDS):
            for t in range(fields[i].shape[0]):
                fields[i][t, 0] = jnp.zeros((ny, nz), jnp.float32)

    @pl.when(sx == n_sx - 1)
    def _():
        for i in range(FIELDS):
            for t in range(fields[i].shape[0]):
                fields[i][t, nx + 1] = jnp.zeros((ny, nz), jnp.float32)

    @pl.when(sy == 0)
    def _():
        for i in range(FIELDS):
            yrecv[i][0] = jnp.zeros(yrecv[i].shape[1:], jnp.float32)

    @pl.when(sy == n_sy - 1)
    def _():
        for i in range(FIELDS):
            yrecv[i][1] = jnp.zeros(yrecv[i].shape[1:], jnp.float32)

    @pl.when(tm == 0)
    def _():
        def clear(x):
            for i in range(7):
                before[i, x] = jnp.zeros((ny, nz), jnp.float32)

        over_rows(clear, 1)

    row = lax.broadcasted_iota(jnp.int32, (ny, nz), 0)
    column = lax.broadcasted_iota(jnp.int32, (ny, nz), 1)

    def around(i, t, x):
        field = fields[i]
        here = field[t, x + 1]
        return here, (
            field[t, x + 2],
            field[t, x],
            jnp.where(row == ny - 1, yrecv[i][1, t, pl.ds(x, 1), :], pltpu.roll(here, ny - 1, 0)),
            jnp.where(row == 0, yrecv[i][0, t, pl.ds(x, 1), :], pltpu.roll(here, 1, 0)),
            pltpu.roll(here, nz - 1, 1),
            pltpu.roll(here, 1, 1),
        )

    def beside(i, t, x, g):
        here, sides = around(i, t, x)
        terms = [g[j] * sides[j] for j in range(6)]
        return here, (terms[0] + terms[1]) + (terms[2] + terms[3]) + (terms[4] + terms[5])

    def faces_at(x):
        return [face[j, x] for j in range(6)]

    wait_faces(KAPPA)

    def coefficients(x):
        here, sides = around(KAPPA, 0, x)
        sides = list(sides)
        sides[4] = jnp.where(column == nz - 1, 0.0, sides[4])
        sides[5] = jnp.where(column == 0, 0.0, sides[5])
        g = [0.5 * (here + side) for side in sides]
        total = (g[0] + g[1]) + (g[2] + g[3]) + (g[4] + g[5])
        coupling[x] = total
        g[4] = jnp.where(column == nz - 1, 0.0, g[4])
        g[5] = jnp.where(column == 0, 0.0, g[5])
        for j in range(6):
            face[j, x] = g[j]
        for level in range(4):
            factor[level, x] = relax_weight / (1.0 + (2.0 ** level) * total)

    over_rows(coefficients)
    loads[2].wait()
    wait_faces(INIT)
    wait_last(P_INIT)

    def sweep_first(x):
        g, f = faces_at(x), factor[0, x]
        running = before[P_INIT, x]
        for t in range(steps):
            here, near = beside(INIT, t, x, g)
            running = keep_weight * here + f * (hs[t, x] + near + running)
            put(FIRST, t, x, running)

    phase(sweep_first, FIRST, functools.partial(send_last, P_FIRST))
    wait_faces(FIRST)
    wait_last(P_FIRST)

    def down_one(x):
        g, diagonal, f = faces_at(x), 1.0 + coupling[x], factor[1, x]
        earlier = before[P_FIRST, x]
        running = None
        for m in range(steps // 2):
            total = None
            for t in (2 * m, 2 * m + 1):
                here, near = beside(FIRST, t, x, g)
                value = hs[t, x] + earlier - (diagonal * here - near)
                total = value if total is None else total + value
                earlier = here
            rhs1[m, x] = total
            running = f * total if running is None else f * (total + running)
            put(ERR1, m, x, running)

    phase(down_one, ERR1, functools.partial(send_last, P_ERR1))
    wait_faces(ERR1)
    wait_last(P_ERR1)

    def down_two(x):
        g, diagonal, f = faces_at(x), 1.0 + 2.0 * coupling[x], factor[2, x]
        earlier = before[P_ERR1, x]
        total = None
        for t in range(2):
            here, near = beside(ERR1, t, x, g)
            value = rhs1[t, x] + earlier - (diagonal * here - 2.0 * near)
            total = value if total is None else total + value
            earlier = here
        rhs2[x] = total
        put(ERR2, 0, x, f * total)

    phase(down_two, ERR2, functools.partial(send_last, P_ERR2))
    wait_faces(ERR2)
    if n_tm > 2:
        wait_last(P_ERR2)

    def down_three(x):
        g, diagonal = faces_at(x), 1.0 + 4.0 * coupling[x]
        here, near = beside(ERR2, 0, x, g)
        earlier = here + before[P_ERR2, x] if n_tm > 2 else here
        value = rhs2[x] + jnp.where(even, earlier, 0.0) - (diagonal * here - 4.0 * near)
        mine[x] = value
        if n_tm == 2:
            put(PART, 0, x, factor[3, x] * value)

    def swap(part):
        return pltpu.make_async_remote_copy(
            src_ref=mine.at[halves[part]], dst_ref=theirs.at[halves[part]],
            send_sem=qsend.at[part], recv_sem=qrecv.at[part],
            device_id={"tm": partner}, device_id_type=MESH)

    if n_tm == 2:
        phase(down_three, PART, lambda part: swap(part).start(), True)
    else:
        over_rows(down_three)
        swap(0).start()
        swap(1).start()
    swap(0).wait_recv()
    swap(1).wait_recv()

    def chain_copy(i, field):
        src = field.at[0, pl.ds(1, nx)] if i == 0 else second
        return pltpu.make_async_remote_copy(
            src_ref=src, dst_ref=chain.at[i], send_sem=csend.at[i],
            recv_sem=crecv.at[i], device_id={"tm": tm + 2}, device_id_type=MESH)

    def chain_wait(i):
        if n_tm > 2:
            @pl.when(tm > 1)
            def _():
                chain_copy(i, fields[ERR3]).wait_recv()

            @pl.when(tm < 2)
            def _():
                def clear(x):
                    chain[i, x] = jnp.zeros((ny, nz), jnp.float32)

                over_rows(clear, 1)

    def chain_send(i):
        if n_tm > 2:
            @pl.when(tm < n_tm - 2)
            def _():
                chain_copy(i, fields[ERR3]).start()

    chain_wait(0)

    def coarse_one(x):
        total = mine[x] + theirs[x]
        rhs3[x] = total
        if n_tm > 2:
            total = total + chain[0, x]
        value = factor[3, x] * total
        if n_tm > 2:
            put(ERR3, 0, x, value)
        else:
            fields[ERR3][0, x + 1] = value

    if n_tm > 2:
        phase(coarse_one, ERR3)
        chain_send(0)
        wait_faces(ERR3)
    else:
        over_rows(coarse_one)
        wait_faces(PART, True)
        for edge in (0, nx + 1):
            fields[ERR3][0, edge] = fields[PART][0, edge] + fields[PAIR][0, edge]
        for edge in range(2):
            yrecv[ERR3][edge, 0] = yrecv[PART][edge, 0] + yrecv[PAIR][edge, 0]
    if n_tm == 2:
        wait_last(P_ERR2)
    chain_wait(1)

    def coarse_two(x):
        here, near = beside(ERR3, 0, x, faces_at(x))
        total = rhs3[x] + 8.0 * near
        if n_tm > 2:
            total = total + chain[1, x]
        value = keep_weight * here + factor[3, x] * total
        if n_tm > 2:
            second[x] = value
            earlier = jnp.where(even, chain[1, x], value)
        else:
            earlier = jnp.where(even, 0.0, value)
        mine_next[x] = before[P_ERR2, x] + earlier
        put(FIX2, 0, x, fields[ERR2][0, x + 1] + value)

    mine_next = res.at[0]
    phase(coarse_two, FIX2)
    chain_send(1)
    wait_faces(FIX2)

    def up_two(x):
        here, near = beside(FIX2, 0, x, faces_at(x))
        value = keep_weight * here + factor[2, x] * (rhs2[x] + 4.0 * near + mine_next[x])
        for m in range(2):
            put(FIX1, m, x, fields[ERR1][m, x + 1] + value)

    phase(up_two, FIX1, functools.partial(send_last, P_FIX1))
    wait_faces(FIX1)
    wait_last(P_FIX1)

    def up_one(x):
        g, f = faces_at(x), factor[1, x]
        running = before[P_FIX1, x]
        for m in range(2):
            here, near = beside(FIX1, m, x, g)
            running = keep_weight * here + f * (rhs1[m, x] + 2.0 * near + running)
            for t in (2 * m, 2 * m + 1):
                put(SUM0, t, x, fields[FIRST][t, x + 1] + running)

    phase(up_one, SUM0, functools.partial(send_last, P_SUM0))
    wait_faces(SUM0)
    wait_last(P_SUM0)

    def up_zero(x):
        g, f = faces_at(x), factor[0, x]
        running = before[P_SUM0, x]
        for t in range(steps):
            here, near = beside(SUM0, t, x, g)
            running = keep_weight * here + f * (hs[t, x] + near + running)
            put(SOL, t, x, running)

    phase(up_zero, SOL, functools.partial(send_last, P_SOL))
    out_one = pltpu.make_async_copy(fields[SOL].at[:, pl.ds(1, nx)], sol_hbm, local.at[3])
    out_one.start()
    wait_faces(SOL)
    wait_last(P_SOL)

    def last_defect(x):
        g, diagonal = faces_at(x), 1.0 + coupling[x]
        earlier = before[P_SOL, x]
        for t in range(steps):
            here, near = beside(SOL, t, x, g)
            res[t, x] = hs[t, x] + earlier - (diagonal * here - near)
            earlier = here

    over_rows(last_defect)
    out_two = pltpu.make_async_copy(res, res_hbm, local.at[4])
    out_two.start()

    for i in range(FIELDS):
        if i == PAIR or i == (ERR3 if n_tm == 2 else PART):
            continue
        for side in (XLO, XHI, YLO, YHI):
            @pl.when(has[side])
            def _(i=i, side=side):
                face_copy(i, side).wait_send()
                if i == PART:
                    face_copy(i, side, True).wait_send()

    @pl.when(tm < n_tm - 1)
    def _():
        for i in range(7):
            for part in range(2):
                last_copy(i, part).wait_send()

    swap(0).wait_send()
    swap(1).wait_send()
    if n_tm > 2:
        @pl.when(tm < n_tm - 2)
        def _():
            for i in range(2):
                chain_copy(i, fields[ERR3]).wait_send()

    out_one.wait()
    out_two.wait()


def solution(mesh):
    n_tm, n_sx, n_sy = (mesh.shape[axis] for axis in ("tm", "sx", "sy"))
    f32 = jnp.float32

    def per_device(heat_source, conductivity, initial_iterate):
        steps, nx, ny, nz = heat_source.shape
        depth = (1, steps, steps, steps // 2, 1, 1, 1, steps // 2, steps, steps, 1, 1)
        scratch = [pltpu.VMEM((d, nx + 2, ny, nz), f32) for d in depth]
        scratch += [pltpu.VMEM((2, d, nx, nz), f32) for d in depth] * 2
        cells = (nx, ny, nz)
        dma = pltpu.SemaphoreType.DMA
        scratch += [
            pltpu.VMEM((steps,) + cells, f32),
            pltpu.VMEM((steps,) + cells, f32),
            pltpu.VMEM((7,) + cells, f32),
            pltpu.VMEM(cells, f32),
            pltpu.VMEM((steps // 2,) + cells, f32),
            pltpu.VMEM(cells, f32),
            pltpu.VMEM(cells, f32),
            pltpu.VMEM(cells, f32),
            pltpu.VMEM(cells, f32),
            pltpu.VMEM((2,) + cells, f32),
            pltpu.VMEM((6,) + cells, f32),
            pltpu.VMEM(cells, f32),
            pltpu.VMEM((4,) + cells, f32),
            dma((FIELDS, 4)), dma((FIELDS, 4)), dma((7, 2)), dma((7, 2)),
            dma((2,)), dma((2,)), dma((2,)), dma((2,)), dma((5,)),
        ]
        field = jax.ShapeDtypeStruct(heat_source.shape, f32)
        return pl.pallas_call(
            functools.partial(kernel, n_tm, n_sx, n_sy),
            out_shape=(field, field),
            in_specs=[pl.BlockSpec(memory_space=pltpu.HBM)] * 3,
            out_specs=(pl.BlockSpec(memory_space=pltpu.HBM),) * 2,
            scratch_shapes=scratch,
            compiler_params=pltpu.CompilerParams(
                collective_id=0, has_side_effects=True, vmem_limit_bytes=67043328
            ),
            name="vcycle",
        )(heat_source, conductivity, initial_iterate)

    placed = (P("tm", "sx", "sy", None), P("sx", "sy", None), P("tm", "sx", "sy", None))
    return jax.shard_map(
        per_device,
        mesh=mesh,
        in_specs=placed,
        out_specs=(P("tm", "sx", "sy", None), P("tm", "sx", "sy", None)),
        check_vma=False,
    )
```

```python
import functools

import jax
import jax.numpy as jnp
from jax import lax
from jax.experimental import pallas as pl
from jax.experimental.pallas import tpu as pltpu
from jax.sharding import PartitionSpec as P

relax_weight = 0.8
keep_weight = 1.0 - relax_weight
MESH = pl.DeviceIdType.MESH

KAPPA, INIT, FIRST, ERR1, ERR2, ERR3, FIX2, FIX1, SUM0, SOL, PART, PAIR, PART2, PAIR2 = range(14)
FIELDS = 14
P_INIT, P_FIRST, P_ERR1, P_ERR2, P_FIX1, P_SUM0, P_SOL = range(7)
XLO, XHI, YLO, YHI = range(4)


def kernel(n_tm, n_sx, n_sy, hs_hbm, k_hbm, in_hbm, sol_hbm, res_hbm, *scratch):
    fields = scratch[:FIELDS]
    yrecv = scratch[FIELDS:2 * FIELDS]
    ysend = scratch[2 * FIELDS:3 * FIELDS]
    (hs, res, before, second, rhs1, rhs2, rhs3, mine, theirs, chain,
     face, coupling, factor, send_sem, recv_sem, tsend, trecv,
     qsend, qrecv, csend, crecv, local) = scratch[3 * FIELDS:]
    steps, nx, ny, nz = hs.shape
    tm, sx, sy = lax.axis_index("tm"), lax.axis_index("sx"), lax.axis_index("sy")
    has = (sx > 0, sx < n_sx - 1, sy > 0, sy < n_sy - 1)
    partner = tm + 1 - 2 * lax.rem(tm, 2)
    even = lax.rem(tm, 2) == 0

    loads = [
        pltpu.make_async_copy(k_hbm, fields[KAPPA].at[0, pl.ds(1, nx)], local.at[0]),
        pltpu.make_async_copy(in_hbm, fields[INIT].at[:, pl.ds(1, nx)], local.at[1]),
        pltpu.make_async_copy(hs_hbm, hs, local.at[2]),
    ]
    for load in loads:
        load.start()

    barrier = pltpu.get_barrier_semaphore()
    greet = [
        (has[XLO], {"sx": sx - 1}), (has[XHI], {"sx": sx + 1}),
        (has[YLO], {"sy": sy - 1}), (has[YHI], {"sy": sy + 1}),
        (tm > 0, {"tm": tm - 1}), (tm < n_tm - 1, {"tm": tm + 1}),
    ]
    if n_tm == 2:
        greet += [
            (has[XLO], {"tm": partner, "sx": sx - 1}), (has[XHI], {"tm": partner, "sx": sx + 1}),
            (has[YLO], {"tm": partner, "sy": sy - 1}), (has[YHI], {"tm": partner, "sy": sy + 1}),
        ]
    if n_tm > 2:
        greet += [(tm > 1, {"tm": tm - 2}), (tm < n_tm - 2, {"tm": tm + 2})]
    count = jnp.int32(0)
    for there, device in greet:
        count = count + jnp.where(there, 1, 0)

        @pl.when(there)
        def _(device=device):
            pl.semaphore_signal(barrier, inc=1, device_id=device, device_id_type=MESH)

    pl.semaphore_wait(barrier, count)

    def face_copy(i, side, pair=False):
        field = fields[i]
        to = i + 1 if pair else i
        land = fields[to]
        if side == XLO:
            if i == INIT:
                src = in_hbm.at[:, pl.ds(0, 1)]
            elif i == KAPPA:
                src = k_hbm.at[pl.ds(0, 1)]
            else:
                src = field.at[:, pl.ds(1, 1)]
            dst, device = land.at[:, pl.ds(nx + 1, 1)], {"sx": sx - 1}
        elif side == XHI:
            if i == INIT:
                src = in_hbm.at[:, pl.ds(nx - 1, 1)]
            elif i == KAPPA:
                src = k_hbm.at[pl.ds(nx - 1, 1)]
            else:
                src = field.at[:, pl.ds(nx, 1)]
            dst, device = land.at[:, pl.ds(0, 1)], {"sx": sx + 1}
        elif side == YLO:
            src, dst, device = ysend[i].at[0], yrecv[to].at[1], {"sy": sy - 1}
        else:
            src, dst, device = ysend[i].at[1], yrecv[to].at[0], {"sy": sy + 1}
        if i == KAPPA and side in (XLO, XHI):
            dst = field.at[0, pl.ds(nx + 1 if side == XLO else 0, 1)]
        if pair:
            device["tm"] = partner
        return pltpu.make_async_remote_copy(
            src_ref=src, dst_ref=dst, send_sem=send_sem.at[to, side],
            recv_sem=recv_sem.at[to, side], device_id=device, device_id_type=MESH)

    def send_faces(i, sides, pair=False):
        for side in sides:
            @pl.when(has[side])
            def _(side=side):
                face_copy(i, side).start()
                if pair:
                    face_copy(i, side, True).start()

    def wait_faces(i, pair=False):
        for side in (YLO, YHI, XLO, XHI):
            @pl.when(has[side ^ 1])
            def _(side=side):
                face_copy(i, side, pair).wait_recv()

    half = nx // 2
    halves = (pl.ds(0, half), pl.ds(half, nx - half))

    def last_copy(i, part):
        field = fields[lasts[i]]
        if i == P_INIT:
            src = in_hbm.at[steps - 1, halves[part]]
        else:
            src = field.at[field.shape[0] - 1, (pl.ds(1, half), pl.ds(1 + half, nx - half))[part]]
        return pltpu.make_async_remote_copy(
            src_ref=src, dst_ref=before.at[i, halves[part]],
            send_sem=tsend.at[i, part], recv_sem=trecv.at[i, part],
            device_id={"tm": tm + 1}, device_id_type=MESH)

    lasts = (INIT, FIRST, ERR1, ERR2, FIX1, SUM0, SOL)

    def send_last(i, part):
        @pl.when(tm < n_tm - 1)
        def _():
            last_copy(i, part).start()

    def wait_last(i, parts=(0, 1)):
        @pl.when(tm > 0)
        def _():
            for part in parts:
                last_copy(i, part).wait_recv()

    send_faces(KAPPA, (XLO, XHI))
    send_faces(INIT, (XLO, XHI))
    send_last(P_INIT, 0)
    send_last(P_INIT, 1)

    def over_rows(body, by=8, start=0, stop=nx):
        def step(x, carry):
            body(x)
            return carry

        lax.fori_loop(start, stop, step, 0, unroll=by)

    def phase(body, i, send_part=None, pair=False, awaited=None):
        if awaited is not None:
            wait_last(awaited, (0,))
        body(0)
        if awaited is None:
            body(nx - 1)
            send_faces(i, (XLO, XHI), pair)
        else:
            send_faces(i, (XLO,), pair)
        over_rows(body, half - 1, 1, half)
        if send_part is not None:
            send_part(0)
        if awaited is not None:
            wait_last(awaited, (1,))
            body(nx - 1)
            send_faces(i, (XHI,), pair)
        over_rows(body, half - 1, half, nx - 1)
        send_faces(i, (YLO, YHI), pair)
        if send_part is not None:
            send_part(1)

    def put_faces(i, t, x, value):
        ysend[i][0, t, pl.ds(x, 1), :] = value[0:1, :]
        ysend[i][1, t, pl.ds(x, 1), :] = value[ny - 1:ny, :]

    def put(i, t, x, value):
        fields[i][t, x + 1] = value
        put_faces(i, t, x, value)

    loads[0].wait()
    loads[1].wait()

    def pack(x):
        put_faces(KAPPA, 0, x, fields[KAPPA][0, x + 1])
        for t in range(steps):
            put_faces(INIT, t, x, fields[INIT][t, x + 1])

    over_rows(pack)
    send_faces(KAPPA, (YLO, YHI))
    send_faces(INIT, (YLO, YHI))

    @pl.when(sx == 0)
    def _():
        for i in range(FIELDS):
            for t in range(fields[i].shape[0]):
                fields[i][t, 0] = jnp.zeros((ny, nz), jnp.float32)

    @pl.when(sx == n_sx - 1)
    def _():
        for i in range(FIELDS):
            for t in range(fields[i].shape[0]):
                fields[i][t, nx + 1] = jnp.zeros((ny, nz), jnp.float32)

    @pl.when(sy == 0)
    def _():
        for i in range(FIELDS):
            yrecv[i][0] = jnp.zeros(yrecv[i].shape[1:], jnp.float32)

    @pl.when(sy == n_sy - 1)
    def _():
        for i in range(FIELDS):
            yrecv[i][1] = jnp.zeros(yrecv[i].shape[1:], jnp.float32)

    @pl.when(tm == 0)
    def _():
        def clear(x):
            for i in range(7):
                before[i, x] = jnp.zeros((ny, nz), jnp.float32)

        over_rows(clear, 1)

    row = lax.broadcasted_iota(jnp.int32, (ny, nz), 0)
    column = lax.broadcasted_iota(jnp.int32, (ny, nz), 1)

    def around(i, t, x):
        field = fields[i]
        here = field[t, x + 1]
        return here, (
            field[t, x + 2],
            field[t, x],
            jnp.where(row == ny - 1, yrecv[i][1, t, pl.ds(x, 1), :], pltpu.roll(here, ny - 1, 0)),
            jnp.where(row == 0, yrecv[i][0, t, pl.ds(x, 1), :], pltpu.roll(here, 1, 0)),
            pltpu.roll(here, nz - 1, 1),
            pltpu.roll(here, 1, 1),
        )

    def beside(i, t, x, g):
        here, sides = around(i, t, x)
        terms = [g[j] * sides[j] for j in range(6)]
        return here, (terms[0] + terms[1]) + (terms[2] + terms[3]) + (terms[4] + terms[5])

    def faces_at(x):
        return [face[j, x] for j in range(6)]

    wait_faces(KAPPA)

    def coefficients(x):
        here, sides = around(KAPPA, 0, x)
        sides = list(sides)
        sides[4] = jnp.where(column == nz - 1, 0.0, sides[4])
        sides[5] = jnp.where(column == 0, 0.0, sides[5])
        g = [0.5 * (here + side) for side in sides]
        total = (g[0] + g[1]) + (g[2] + g[3]) + (g[4] + g[5])
        coupling[x] = total
        g[4] = jnp.where(column == nz - 1, 0.0, g[4])
        g[5] = jnp.where(column == 0, 0.0, g[5])
        for j in range(6):
            face[j, x] = g[j]
        for level in range(4):
            factor[level, x] = relax_weight / (1.0 + (2.0 ** level) * total)

    over_rows(coefficients)
    loads[2].wait()
    wait_faces(INIT)

    def sweep_first(x):
        g, f = faces_at(x), factor[0, x]
        running = before[P_INIT, x]
        for t in range(steps):
            here, near = beside(INIT, t, x, g)
            running = keep_weight * here + f * (hs[t, x] + near + running)
            put(FIRST, t, x, running)

    phase(sweep_first, FIRST, functools.partial(send_last, P_FIRST), awaited=P_INIT)
    wait_faces(FIRST)

    def down_one(x):
        g, diagonal, f = faces_at(x), 1.0 + coupling[x], factor[1, x]
        earlier = before[P_FIRST, x]
        running = None
        for m in range(steps // 2):
            total = None
            for t in (2 * m, 2 * m + 1):
                here, near = beside(FIRST, t, x, g)
                value = hs[t, x] + earlier - (diagonal * here - near)
                total = value if total is None else total + value
                earlier = here
            rhs1[m, x] = total
            running = f * total if running is None else f * (total + running)
            put(ERR1, m, x, running)

    phase(down_one, ERR1, functools.partial(send_last, P_ERR1), awaited=P_FIRST)
    wait_faces(ERR1)
    wait_last(P_ERR1)

    def down_two(x):
        g, diagonal, f = faces_at(x), 1.0 + 2.0 * coupling[x], factor[2, x]
        earlier = before[P_ERR1, x]
        total = None
        for t in range(2):
            here, near = beside(ERR1, t, x, g)
            value = rhs1[t, x] + earlier - (diagonal * here - 2.0 * near)
            total = value if total is None else total + value
            earlier = here
        rhs2[x] = total
        put(ERR2, 0, x, f * total)

    phase(down_two, ERR2, functools.partial(send_last, P_ERR2))
    wait_faces(ERR2)
    if n_tm > 2:
        wait_last(P_ERR2)

    def down_three(x):
        g, diagonal = faces_at(x), 1.0 + 4.0 * coupling[x]
        here, near = beside(ERR2, 0, x, g)
        earlier = here + before[P_ERR2, x] if n_tm > 2 else here
        value = rhs2[x] + jnp.where(even, earlier, 0.0) - (diagonal * here - 4.0 * near)
        mine[x] = value
        if n_tm == 2:
            put(PART, 0, x, factor[3, x] * value)

    def swap(part):
        return pltpu.make_async_remote_copy(
            src_ref=mine.at[halves[part]], dst_ref=theirs.at[halves[part]],
            send_sem=qsend.at[part], recv_sem=qrecv.at[part],
            device_id={"tm": partner}, device_id_type=MESH)

    if n_tm == 2:
        phase(down_three, PART, lambda part: swap(part).start(), True)
        wait_faces(PART)

        def part_two(x):
            here, near = beside(PART, 0, x, faces_at(x))
            put(PART2, 0, x, keep_weight * here + factor[3, x] * (mine[x] + 8.0 * near))

        phase(part_two, PART2, None, True)
    else:
        over_rows(down_three)
        swap(0).start()
        swap(1).start()
    swap(0).wait_recv()
    swap(1).wait_recv()

    def chain_copy(i, field):
        src = field.at[0, pl.ds(1, nx)] if i == 0 else second
        return pltpu.make_async_remote_copy(
            src_ref=src, dst_ref=chain.at[i], send_sem=csend.at[i],
            recv_sem=crecv.at[i], device_id={"tm": tm + 2}, device_id_type=MESH)

    def chain_wait(i):
        if n_tm > 2:
            @pl.when(tm > 1)
            def _():
                chain_copy(i, fields[ERR3]).wait_recv()

            @pl.when(tm < 2)
            def _():
                def clear(x):
                    chain[i, x] = jnp.zeros((ny, nz), jnp.float32)

                over_rows(clear, 1)

    def chain_send(i):
        if n_tm > 2:
            @pl.when(tm < n_tm - 2)
            def _():
                chain_copy(i, fields[ERR3]).start()

    chain_wait(0)

    def coarse_one(x):
        total = mine[x] + theirs[x]
        rhs3[x] = total
        if n_tm > 2:
            total = total + chain[0, x]
        value = factor[3, x] * total
        if n_tm > 2:
            put(ERR3, 0, x, value)
        else:
            fields[ERR3][0, x + 1] = value

    if n_tm > 2:
        phase(coarse_one, ERR3)
        chain_send(0)
        wait_faces(ERR3)
    else:
        over_rows(coarse_one)
        wait_faces(PART, True)
        for edge in (0, nx + 1):
            fields[ERR3][0, edge] = fields[PART][0, edge] + fields[PAIR][0, edge]
        for edge in range(2):
            yrecv[ERR3][edge, 0] = yrecv[PART][edge, 0] + yrecv[PAIR][edge, 0]
    if n_tm == 2:
        wait_last(P_ERR2)
    chain_wait(1)

    def coarse_two(x):
        here, near = beside(ERR3, 0, x, faces_at(x))
        total = rhs3[x] + 8.0 * near
        if n_tm > 2:
            total = total + chain[1, x]
        value = keep_weight * here + factor[3, x] * total
        if n_tm > 2:
            second[x] = value
            earlier = jnp.where(even, chain[1, x], value)
        else:
            earlier = jnp.where(even, 0.0, value)
        mine_next[x] = before[P_ERR2, x] + earlier
        value = fields[ERR2][0, x + 1] + value
        if n_tm > 2:
            put(FIX2, 0, x, value)
        else:
            fields[FIX2][0, x + 1] = value

    mine_next = res.at[0]
    if n_tm > 2:
        phase(coarse_two, FIX2)
        chain_send(1)
        wait_faces(FIX2)
    else:
        over_rows(coarse_two)
        wait_faces(PART2)
        wait_faces(PART2, True)
        for edge in (0, nx + 1):
            fields[FIX2][0, edge] = fields[ERR2][0, edge] + (
                fields[PART2][0, edge] + fields[PAIR2][0, edge])
        for edge in range(2):
            yrecv[FIX2][edge, 0] = yrecv[ERR2][edge, 0] + (
                yrecv[PART2][edge, 0] + yrecv[PAIR2][edge, 0])

    def up_two(x):
        here, near = beside(FIX2, 0, x, faces_at(x))
        value = keep_weight * here + factor[2, x] * (rhs2[x] + 4.0 * near + mine_next[x])
        for m in range(2):
            put(FIX1, m, x, fields[ERR1][m, x + 1] + value)

    phase(up_two, FIX1, functools.partial(send_last, P_FIX1))
    wait_faces(FIX1)

    def up_one(x):
        g, f = faces_at(x), factor[1, x]
        running = before[P_FIX1, x]
        for m in range(2):
            here, near = beside(FIX1, m, x, g)
            running = keep_weight * here + f * (rhs1[m, x] + 2.0 * near + running)
            for t in (2 * m, 2 * m + 1):
                put(SUM0, t, x, fields[FIRST][t, x + 1] + running)

    phase(up_one, SUM0, functools.partial(send_last, P_SUM0), awaited=P_FIX1)
    wait_faces(SUM0)
    wait_last(P_SUM0)

    def up_zero(x):
        g, f = faces_at(x), factor[0, x]
        running = before[P_SUM0, x]
        for t in range(steps):
            here, near = beside(SUM0, t, x, g)
            running = keep_weight * here + f * (hs[t, x] + near + running)
            put(SOL, t, x, running)

    phase(up_zero, SOL, functools.partial(send_last, P_SOL))
    out_one = pltpu.make_async_copy(fields[SOL].at[:, pl.ds(1, nx)], sol_hbm, local.at[3])
    out_one.start()
    wait_faces(SOL)
    wait_last(P_SOL)

    def last_defect(x):
        g, diagonal = faces_at(x), 1.0 + coupling[x]
        earlier = before[P_SOL, x]
        for t in range(steps):
            here, near = beside(SOL, t, x, g)
            res[t, x] = hs[t, x] + earlier - (diagonal * here - near)
            earlier = here

    over_rows(last_defect)
    out_two = pltpu.make_async_copy(res, res_hbm, local.at[4])
    out_two.start()

    for i in range(FIELDS):
        if i in ((PAIR, PAIR2, ERR3, FIX2) if n_tm == 2 else (PART, PAIR, PART2, PAIR2)):
            continue
        for side in (XLO, XHI, YLO, YHI):
            @pl.when(has[side])
            def _(i=i, side=side):
                face_copy(i, side).wait_send()
                if i in (PART, PART2):
                    face_copy(i, side, True).wait_send()

    @pl.when(tm < n_tm - 1)
    def _():
        for i in range(7):
            for part in range(2):
                last_copy(i, part).wait_send()

    swap(0).wait_send()
    swap(1).wait_send()
    if n_tm > 2:
        @pl.when(tm < n_tm - 2)
        def _():
            for i in range(2):
                chain_copy(i, fields[ERR3]).wait_send()

    out_one.wait()
    out_two.wait()


def solution(mesh):
    n_tm, n_sx, n_sy = (mesh.shape[axis] for axis in ("tm", "sx", "sy"))
    f32 = jnp.float32

    def per_device(heat_source, conductivity, initial_iterate):
        steps, nx, ny, nz = heat_source.shape
        depth = (1, steps, steps, steps // 2, 1, 1, 1, steps // 2, steps, steps, 1, 1, 1, 1)
        scratch = [pltpu.VMEM((d, nx + 2, ny, nz), f32) for d in depth]
        scratch += [pltpu.VMEM((2, d, nx, nz), f32) for d in depth] * 2
        cells = (nx, ny, nz)
        dma = pltpu.SemaphoreType.DMA
        scratch += [
            pltpu.VMEM((steps,) + cells, f32),
            pltpu.VMEM((steps,) + cells, f32),
            pltpu.VMEM((7,) + cells, f32),
            pltpu.VMEM(cells, f32),
            pltpu.VMEM((steps // 2,) + cells, f32),
            pltpu.VMEM(cells, f32),
            pltpu.VMEM(cells, f32),
            pltpu.VMEM(cells, f32),
            pltpu.VMEM(cells, f32),
            pltpu.VMEM((2,) + cells, f32),
            pltpu.VMEM((6,) + cells, f32),
            pltpu.VMEM(cells, f32),
            pltpu.VMEM((4,) + cells, f32),
            dma((FIELDS, 4)), dma((FIELDS, 4)), dma((7, 2)), dma((7, 2)),
            dma((2,)), dma((2,)), dma((2,)), dma((2,)), dma((5,)),
        ]
        field = jax.ShapeDtypeStruct(heat_source.shape, f32)
        return pl.pallas_call(
            functools.partial(kernel, n_tm, n_sx, n_sy),
            out_shape=(field, field),
            in_specs=[pl.BlockSpec(memory_space=pltpu.HBM)] * 3,
            out_specs=(pl.BlockSpec(memory_space=pltpu.HBM),) * 2,
            scratch_shapes=scratch,
            compiler_params=pltpu.CompilerParams(
                collective_id=0, has_side_effects=True, vmem_limit_bytes=67043328
            ),
            name="vcycle",
        )(heat_source, conductivity, initial_iterate)

    placed = (P("tm", "sx", "sy", None), P("sx", "sy", None), P("tm", "sx", "sy", None))
    return jax.shard_map(
        per_device,
        mesh=mesh,
        in_specs=placed,
        out_specs=(P("tm", "sx", "sy", None), P("tm", "sx", "sy", None)),
        check_vma=False,
    )
```
